32 devices in a mesh: fsdp: 8 (over z, core), tp: 4 (over y, x).
Axes of the slice: x: 2, y: 2, z: 4, core: 2. Of those that a mesh axis runs over, the one named last changes fastest.
Arguments:
- tokens: bfloat16 [14336, 1536], P(('fsdp', 'tp')), may hold values from -6 to 6
- gain_one: float32 [1536], P(('fsdp', 'tp')), may hold values from 0.5 to 1.5
- in_weight: bfloat16 [1536, 3, 1536], P('fsdp', None, 'tp'), may hold values from -0.15625 to 0.15625
- conv_weight: bfloat16 [3, 1536], P(None, ('tp', 'fsdp')), may hold values from -3.5 to 3.5
- out_weight: bfloat16 [1536, 1536], P('tp', 'fsdp'), may hold values from -0.15625 to 0.15625
- gain_two: float32 [1536], P(('fsdp', 'tp')), may hold values from 0.5 to 1.5
- gate_up_weight: bfloat16 [1536, 2, 6912], P('fsdp', None, 'tp'), may hold values from -0.15625 to 0.15625
- down_weight: bfloat16 [6912, 1536], P('tp', 'fsdp'), may hold values from -0.078125 to 0.078125
- cotangent: bfloat16 [14336, 1536], P(('fsdp', 'tp')), may hold values from -6 to 6
- lengths: int32 [8], replicated, may hold values from 448 to 1792, as said below
Outputs:
- output: bfloat16 [14336, 1536], P(('fsdp', 'tp'))
- input_grad: bfloat16 [14336, 1536], P(('fsdp', 'tp'))
- gain_one_grad: float32 [1536], P(('fsdp', 'tp'))
- in_weight_grad: float32 [1536, 3, 1536], P('fsdp', None, 'tp')
- conv_weight_grad: float32 [3, 1536], P(None, ('tp', 'fsdp'))
- out_weight_grad: float32 [1536, 1536], P('tp', 'fsdp')
- gain_two_grad: float32 [1536], P(('fsdp', 'tp'))
- gate_up_grad: float32 [1536, 2, 6912], P('fsdp', None, 'tp')
- down_grad: float32 [6912, 1536], P('tp', 'fsdp')
- out_rms: float32 [8, 1536], P('fsdp', 'tp')
The draws below stay inside these ranges and needn't reach their ends.
Inputs may be any that keep to these rules, and one draw needn't show every extreme that they name: `lengths`: some slot has exactly 1792 valid tokens and another exactly 448.
All inputs are finite; a program needn't handle non-finite values.
Results may differ from the reference program's by a relative error of at most 0.023.
Values may be sent and summed in bfloat16 or wider, within the bound.
No kernel may reach another device: no remote copies, remote signals or barrier semaphores. Data moves between devices by JAX's collectives and lax.ppermute only.
A program may use at most 256 MiB of HBM per device.

```python
import jax
import jax.numpy as jnp
from jax import lax

D = 1536
FF = 6912
CONV_WIDTH = 3
SLOT = 1792
SLOTS = 8
LEN_MIN = 448
TOKENS = 14336


def draw_lengths(key, part):
    first, second, third = jax.random.split(jax.random.fold_in(key, 7), 3)
    values = jax.random.randint(first, (SLOTS,), LEN_MIN, SLOT + 1)
    longest = jax.random.randint(second, (), 0, SLOTS)
    offset = jax.random.randint(third, (), 1, SLOTS)
    shortest = (longest + offset) % SLOTS
    slot_index = jnp.arange(SLOTS)
    values = jnp.where(slot_index == longest, SLOT, values)
    values = jnp.where(slot_index == shortest, LEN_MIN, values)
    return values.astype(jnp.int32)


def shard_levels(stream_key, shape, cuts, least, top_value):
    def one(dim, shards_of):
        heights = jax.random.uniform(jax.random.fold_in(jax.random.fold_in(stream_key, 6), dim), (shards_of,), jnp.float32, least / len(cuts), top_value / len(cuts))
        return jnp.repeat(jnp.exp(heights), shape[dim] // shards_of).reshape((-1,) + (1,) * (len(shape) - dim - 1))

    factor_of = one(*cuts[0])
    for cut in cuts[1:]:
        factor_of = factor_of * one(*cut)
    return factor_of


def scatter_about(key, dims, width, bound, cuts=(), held_as=jnp.bfloat16):
    result = width * jax.random.normal(key, dims, jnp.float32)
    if cuts:
        result = result * shard_levels(key, dims, cuts, -0.22, 0.18)
    return jnp.clip(result, -bound, bound).astype(held_as)


def setup_inputs(seed: int = 0) -> dict:
    arg_keys = jax.random.split(jax.random.key(seed), 11)
    return {
        "tokens": scatter_about(arg_keys[0], (TOKENS, D), 1.0, 6.0, ((0, 32),)),
        "gain_one": jnp.clip(1.0 + 0.1 * jax.random.normal(arg_keys[1], (D,), jnp.float32), 0.5, 1.5),
        "in_weight": scatter_about(arg_keys[2], (D, 3, D), D ** -0.5, 0.15625, ((0, 8), (2, 4))),
        "conv_weight": scatter_about(arg_keys[3], (CONV_WIDTH, D), 3 ** -0.5, 3.5, ((1, 32),)),
        "out_weight": scatter_about(arg_keys[4], (D, D), D ** -0.5, 0.15625, ((0, 4), (1, 8))),
        "gain_two": jnp.clip(1.0 + 0.1 * jax.random.normal(arg_keys[5], (D,), jnp.float32), 0.5, 1.5),
        "gate_up_weight": scatter_about(arg_keys[6], (D, 2, FF), D ** -0.5, 0.15625, ((0, 8), (2, 4))),
        "down_weight": scatter_about(arg_keys[7], (FF, D), FF ** -0.5, 0.078125, ((0, 4), (1, 8))),
        "cotangent": scatter_about(arg_keys[8], (TOKENS, D), 1.0, 6.0, ((0, 32),)),
        "lengths": draw_lengths(jax.random.fold_in(arg_keys[10], 71), 0),
    }


@jax.custom_vjp
def low(v):
    return lax.optimization_barrier(v.astype(jnp.bfloat16)).astype(jnp.float32)

@jax.custom_vjp
def low_back(v):
    return v

def low_keep(v):
    return (low(v), None)

def low_pass(kept, grad):
    return (grad,)

def back_keep(v):
    return (v, None)

def back_low(kept, grad):
    return (low(grad),)
low.defvjp(low_keep, low_pass)
low_back.defvjp(back_keep, back_low)
EPSILON = 1e-05
HIGHEST = lax.Precision.HIGHEST

def rms_norm(values, gain):
    scale = lax.rsqrt(lax.optimization_barrier(jnp.mean(values * values, axis=-1, keepdims=True)) + EPSILON)
    return values * scale * gain

def conv_block(inputs, gain_one, in_weight, conv_weight, out_weight, gain_two, gate_up_weight, down_weight):
    normed = low(rms_norm(inputs, gain_one))
    projected = low_back(jnp.einsum('td,dkc->tkc', normed, in_weight, precision=HIGHEST))
    input_gate = projected[:, 0]
    output_gate = projected[:, 1]
    inner_values = projected[:, 2]
    mixed_values = input_gate * inner_values
    padded = jnp.pad(mixed_values, ((2, 0), (0, 0)))
    convolved = conv_weight[0] * padded[:-2] + conv_weight[1] * padded[1:-1] + conv_weight[2] * padded[2:]
    gated = low(output_gate * convolved)
    branch = low_back(jnp.dot(gated, out_weight, precision=HIGHEST))
    hidden = inputs + branch
    normed_two = low(rms_norm(hidden, gain_two))
    gate_up = low_back(jnp.einsum('td,dkf->tkf', normed_two, gate_up_weight, precision=HIGHEST))
    activated = low(jax.nn.silu(gate_up[:, 0]) * gate_up[:, 1])
    ffn_out = low_back(jnp.dot(activated, down_weight, precision=HIGHEST))
    return hidden + ffn_out

def reference(tokens, gain_one, in_weight, conv_weight, out_weight, gain_two, gate_up_weight, down_weight, cotangent, lengths):
    weights = tuple((w.astype(jnp.float32) for w in (gain_one, in_weight, conv_weight, out_weight, gain_two, gate_up_weight, down_weight)))
    inputs = tokens.astype(jnp.float32).reshape(SLOTS, SLOT, D)
    cots = cotangent.astype(jnp.float32).reshape(SLOTS, SLOT, D)
    position = jnp.arange(SLOT)

    def per_sequence(totals, sequence_item):
        sequence, seq_cot, length = sequence_item
        valid_mask = (position < length).astype(jnp.float32)[:, None]
        full_out, pullback = jax.vjp(conv_block, sequence, *weights)
        gradients = pullback(seq_cot * valid_mask)
        totals = tuple((a + b for a, b in zip(totals, gradients[1:])))
        squares = lax.optimization_barrier(jnp.sum(full_out * full_out * valid_mask, axis=0))
        out_rms = jnp.sqrt(squares / length.astype(jnp.float32))
        return (totals, (full_out.astype(jnp.bfloat16), gradients[0].astype(jnp.bfloat16), out_rms))
    zeros = tuple((jnp.zeros_like(w) for w in weights))
    totals, (outputs, input_grads, rms_values) = lax.scan(per_sequence, zeros, (inputs, cots, lengths))
    output = outputs.reshape(TOKENS, D)
    input_grad = input_grads.reshape(TOKENS, D)
    return (output, input_grad, totals[0], totals[1], totals[2], totals[3], totals[4], totals[5], totals[6], rms_values)
```

```python
import jax
import jax.numpy as jnp
from jax import lax
from jax.experimental.layout import Layout, with_layout_constraint
from jax.sharding import PartitionSpec as P


EPSILON = 1e-05
F32 = jnp.float32
BF16 = jnp.bfloat16


def flip(value, axis, size, mask):
    return lax.ppermute(value, axis, [(i, i ^ mask) for i in range(size)])


def bits_of(size):
    return [1 << b for b in range(size.bit_length() - 1)]


def gather_small(value, axis, size):
    value = value[None]
    index = lax.axis_index(axis)
    for bit in bits_of(size):
        other = flip(value, axis, size, bit)
        high = (index & bit) != 0
        value = jnp.where(
            high, jnp.concatenate([other, value], 0), jnp.concatenate([value, other], 0)
        )
    return value


def scatter_small(value, axis, size):
    index = lax.axis_index(axis)
    for bit in reversed(bits_of(size)):
        half = value.shape[0] // 2
        high = (index & bit) != 0
        mine = jnp.where(high, value[half:], value[:half])
        other = jnp.where(high, value[:half], value[half:])
        value = mine + flip(other, axis, size, bit)
    return value[0]


def spread(piece, size, late=None):
    half = piece.shape[0] // 2
    if size == 4:
        near_x = flip(piece, "tp", size, 1)
        near_y = flip(piece, "tp", size, 2)
        if late is not None:
            near_x, near_y = after(late(), near_x, near_y)
        far_a = flip(near_x[:half], "tp", size, 2)
        far_b = flip(near_y[half:], "tp", size, 1)
        return [piece, near_x, near_y, (far_a, far_b)]
    held = {0: piece}
    for bit in bits_of(size):
        for mask in sorted(held):
            held[mask | bit] = flip(held[mask], "tp", size, bit)
    return [held[m] for m in range(size)]


def last_of(pieces):
    return pieces[-1][0] if isinstance(pieces[-1], tuple) else pieces[-1]


def join(pieces):
    flat = []
    for p in pieces:
        flat.extend(p if isinstance(p, tuple) else (p,))
    return jnp.concatenate(flat, axis=0)


def collect(parts, size):
    half = parts[0].shape[0] // 2
    if size == 4:
        send_x = jnp.concatenate([parts[3][:half], parts[1][:half]], 0)
        send_y = jnp.concatenate([parts[3][half:], parts[2][half:]], 0)
        got_x = flip(send_x, "tp", size, 1)
        got_y = flip(send_y, "tp", size, 2)
        next_y = (parts[2][:half].astype(F32) + got_x[:half].astype(F32)).astype(BF16)
        next_x = (parts[1][half:].astype(F32) + got_y[:half].astype(F32)).astype(BF16)
        last_y = flip(next_y, "tp", size, 2)
        last_x = flip(next_x, "tp", size, 1)
        top = parts[0][:half].astype(F32) + got_x[half:].astype(F32) + last_y.astype(F32)
        low = parts[0][half:].astype(F32) + got_y[half:].astype(F32) + last_x.astype(F32)
        return jnp.concatenate([top, low], 0)
    held = {m: parts[m] for m in range(size)}
    for bit in reversed(bits_of(size)):
        for mask in [m for m in sorted(held) if m & bit]:
            got = flip(held.pop(mask), "tp", size, bit)
            low = mask ^ bit
            held[low] = (held[low].astype(F32) + got.astype(F32)).astype(BF16)
    return held[0].astype(F32)


def dot_rows(left, right):
    return lax.dot_general(left, right, (((0,), (0,)), ((), ())), preferred_element_type=F32)


def dot_cols(left, right):
    return lax.dot_general(left, right, (((1,), (1,)), ((), ())), preferred_element_type=F32)


def planes(value):
    return with_layout_constraint(value, Layout(major_to_minor=(1, 0, 2)))


def after(done, *values):
    held = lax.optimization_barrier((done,) + values)
    return held[1] if len(values) == 1 else held[1:]


def build(n_f, n_tp):
    def block(
        tokens,
        gain_one,
        in_weight,
        conv_weight,
        out_weight,
        gain_two,
        gate_up_weight,
        down_weight,
        cotangent,
        lengths,
    ):
        rows, width = tokens.shape
        channels = in_weight.shape[2]
        gain_width = gain_one.shape[0]
        tp_index = lax.axis_index("tp")

        io_local = jnp.concatenate([in_weight, out_weight.T[:, None, :]], axis=1)
        weight_io = planes(lax.all_gather(planes(io_local), "fsdp", axis=0, tiled=True))
        weight_gu = planes(lax.all_gather(planes(gate_up_weight), "fsdp", axis=0, tiled=True))
        weight_down = lax.all_gather(down_weight, "fsdp", axis=1, tiled=True)
        weight_in, weight_out = weight_io[:, :3], weight_io[:, 3]

        inputs = tokens.astype(F32)
        scale_one = lax.rsqrt(jnp.mean(inputs * inputs, axis=1, keepdims=True) + EPSILON)
        plain = (inputs * scale_one).astype(BF16)
        plain_parts = spread(plain, n_tp)

        small = jnp.concatenate([gain_one, gain_two, conv_weight.astype(F32).reshape(-1)])
        small = gather_small(small, "fsdp", n_f)
        taps = (
            small[:, 2 * gain_width :]
            .reshape(n_f, 3, gain_width)
            .transpose(1, 0, 2)
            .reshape(3, channels)
        )
        gains = gather_small(small[:, : 2 * gain_width].reshape(-1), "tp", n_tp)
        gains = gains.reshape(n_tp, n_f, 2, gain_width).transpose(2, 1, 0, 3).reshape(2, width)
        gain_first, gain_second = gains[0], gains[1]

        length = lengths[lax.axis_index("fsdp")]
        position = tp_index * rows + jnp.arange(rows)
        valid_mask = (position < length).astype(F32)[:, None]
        grad_ffn = cotangent.astype(F32) * valid_mask
        cot_piece = after(last_of(plain_parts), grad_ffn.astype(BF16))

        gathered = (join(plain_parts).astype(F32) * gain_first).astype(BF16)
        projected = jnp.einsum("td,dkc->tkc", gathered, weight_in, preferred_element_type=F32)
        projected = projected.reshape(n_tp, rows, 3, channels)
        input_gate, output_gate, inner_values = (projected[:, :, k] for k in range(3))
        mixed = input_gate * inner_values
        slot = jnp.arange(n_tp)
        before_slot = (tp_index ^ slot) - 1
        after_slot = (tp_index ^ slot) + 1

        def edge_of(edge, wanted):
            hits = (wanted[:, None] ^ tp_index) == slot[None, :]
            inside = (wanted >= 0) & (wanted < n_tp)
            hits = hits & inside[:, None]
            return sum(
                jnp.where(hits[:, s][:, None, None], edge[s][None], 0.0) for s in range(n_tp)
            )

        tail = edge_of(mixed[:, -2:], before_slot)
        earlier_one = jnp.concatenate([tail[:, 1:], mixed[:, :-1]], axis=1)
        earlier_two = jnp.concatenate([tail, mixed[:, :-2]], axis=1)
        convolved = taps[0] * earlier_two + taps[1] * earlier_one + taps[2] * mixed
        gated = (output_gate * convolved).astype(BF16).reshape(n_tp * rows, channels)

        def rows_of(value, m):
            return value[m * rows : (m + 1) * rows]

        branch = dot_cols(gated, weight_out).astype(BF16)
        hidden = inputs + collect([rows_of(branch, m) for m in range(n_tp)], n_tp)
        scale_two = lax.rsqrt(jnp.mean(hidden * hidden, axis=1, keepdims=True) + EPSILON)
        normed_two = (hidden * scale_two * gain_second).astype(BF16)
        parts_two = spread(normed_two, n_tp)
        gathered_two = join(parts_two)
        grad_ffn_rows = join(spread(cot_piece, n_tp, lambda: last_of(parts_two)))
        gate_part = jnp.dot(gathered_two, weight_gu[:, 0], preferred_element_type=F32).astype(BF16)
        up_part = jnp.dot(gathered_two, weight_gu[:, 1], preferred_element_type=F32)
        gate_wide = gate_part.astype(F32)
        activated = (gate_wide * jax.nn.sigmoid(gate_wide) * up_part).astype(BF16)
        up_part = up_part.astype(BF16)
        activated, gate_part, up_part = lax.optimization_barrier((activated, gate_part, up_part))

        down_local = with_layout_constraint(
            dot_rows(grad_ffn_rows, activated).astype(BF16).T, Layout(major_to_minor=(1, 0))
        )
        down_grad = lax.psum_scatter(down_local, "fsdp", scatter_dimension=1, tiled=True)
        down_grad = down_grad.astype(F32)

        grad_rows_late, weight_down_late = after(down_local, grad_ffn_rows, weight_down)
        grad_act = dot_cols(grad_rows_late, weight_down_late)
        gate_wide, up_wide = gate_part.astype(F32), up_part.astype(F32)
        sigmoid_gate = jax.nn.sigmoid(gate_wide)
        grad_gate = grad_act * up_wide * sigmoid_gate * (1.0 + gate_wide * (1.0 - sigmoid_gate))
        grad_up = grad_act * gate_wide * sigmoid_gate
        grad_gate, grad_up = grad_gate.astype(BF16), grad_up.astype(BF16)
        grad_gate, grad_up = lax.optimization_barrier((grad_gate, grad_up))

        def split_back(values, weights, between=None):
            def back_of(parts):
                return jnp.einsum(
                    "tkc,dkc->td", jnp.stack(parts, 1), weights, preferred_element_type=F32
                ).astype(BF16)

            others = back_of([v[rows:] for v in values])
            middle = between(others) if between else others
            own = back_of(after(middle, *[v[:rows] for v in values]))
            return [own] + [rows_of(others, m) for m in range(n_tp - 1)], middle

        def gate_up_sum(others):
            local = jnp.einsum(
                "td,tkf->dkf",
                gathered_two,
                jnp.stack(after(others, grad_gate, grad_up), 1),
                preferred_element_type=F32,
            ).astype(BF16)
            return planes(local)

        back_parts, gate_up_local = split_back((grad_gate, grad_up), weight_gu, gate_up_sum)
        grad_normed_two = collect(back_parts, n_tp)
        gate_up_grad = lax.psum_scatter(
            gate_up_local, "fsdp", scatter_dimension=0, tiled=True
        )
        gate_up_grad = gate_up_grad.astype(F32)

        weighted = grad_normed_two * gain_second
        inner_mean = jnp.mean(weighted * hidden, axis=1, keepdims=True)
        gain_two_local = jnp.sum(grad_normed_two * hidden * scale_two, axis=0)
        grad_hidden = (
            grad_ffn + scale_two * weighted - hidden * (scale_two * scale_two * scale_two) * inner_mean
        )
        branch_piece = grad_hidden.astype(BF16)
        branch_parts = spread(branch_piece, n_tp)
        grad_branch_rows = join(branch_parts)

        ffn_sum = jnp.dot(
            after(branch_piece, activated), weight_down, preferred_element_type=F32
        ).astype(BF16)
        ffn_late = after(last_of(branch_parts), ffn_sum)
        full_out = hidden + collect([rows_of(ffn_late, m) for m in range(n_tp)], n_tp)
        output = full_out.astype(BF16)
        squares = jnp.sum(full_out * full_out * valid_mask, axis=0)

        grad_gated = jnp.dot(
            grad_branch_rows, weight_out, preferred_element_type=F32
        ).reshape(n_tp, rows, channels)
        grad_conv = grad_gated * output_gate
        grad_output_gate = grad_gated * convolved
        conv_local = jnp.stack(
            [
                jnp.sum(grad_conv * earlier_two, axis=(0, 1)),
                jnp.sum(grad_conv * earlier_one, axis=(0, 1)),
                jnp.sum(grad_conv * mixed, axis=(0, 1)),
            ],
            axis=0,
        )
        head = edge_of(grad_conv[:, :2], after_slot)
        later_one = jnp.concatenate([grad_conv[:, 1:], head[:, :1]], axis=1)
        later_two = jnp.concatenate([grad_conv[:, 2:], head], axis=1)
        grad_mixed = taps[2] * grad_conv + taps[1] * later_one + taps[0] * later_two
        grad_projected = lax.optimization_barrier(
            tuple(
                v.astype(BF16).reshape(n_tp * rows, channels)
                for v in (grad_mixed * inner_values, grad_output_gate, grad_mixed * input_gate)
            )
        )
        out_local = dot_rows(grad_branch_rows, gated).astype(BF16)
        in_local = jnp.einsum(
            "td,tkc->dkc", gathered, jnp.stack(grad_projected, 1), preferred_element_type=F32
        ).astype(BF16)
        io_sum = planes(jnp.concatenate([in_local, out_local[:, None, :]], axis=1))
        io_grad = lax.psum_scatter(io_sum, "fsdp", scatter_dimension=0, tiled=True)
        io_grad = io_grad.astype(F32)
        in_grad, out_grad = io_grad[:, :3], io_grad[:, 3].T

        first_parts, _ = split_back(after(io_sum, *grad_projected), weight_in)
        grad_normed = collect(first_parts, n_tp)
        weighted_one = grad_normed * gain_first
        inner_one = jnp.mean(weighted_one * inputs, axis=1, keepdims=True)
        gain_one_local = jnp.sum(grad_normed * inputs * scale_one, axis=0)
        input_grad = (
            grad_hidden
            + scale_one * weighted_one
            - inputs * (scale_one * scale_one * scale_one) * inner_one
        ).astype(BF16)

        conv_share = conv_local.reshape(3, n_f, -1).transpose(1, 0, 2).reshape(n_f, -1)
        small_sums = jnp.concatenate([gain_two_local.reshape(n_f, -1), conv_share], axis=1)
        small_sums = scatter_small(after(io_sum, small_sums), "fsdp", n_f)
        two_share, conv_grad = small_sums[: width // n_f], small_sums[width // n_f :]
        conv_grad = conv_grad.reshape(3, -1)
        small_sums = jnp.concatenate([two_share.reshape(n_tp, -1), squares.reshape(n_tp, -1)], 1)
        small_sums = scatter_small(small_sums, "tp", n_tp)
        gain_two_grad, square_share = small_sums[:gain_width], small_sums[gain_width:]
        out_rms = jnp.sqrt(square_share / length.astype(F32))[None, :]
        one_share = scatter_small(gain_one_local.reshape(n_f, -1), "fsdp", n_f)
        gain_one_grad = scatter_small(one_share.reshape(n_tp, -1), "tp", n_tp)
        return (
            output,
            input_grad,
            gain_one_grad,
            in_grad,
            conv_grad,
            out_grad,
            gain_two_grad,
            gate_up_grad,
            down_grad,
            out_rms,
        )

    return block


def solution(mesh):
    rows = P(("fsdp", "tp"), None)
    gains = P(("fsdp", "tp"))
    wide = P("fsdp", None, "tp")
    taps = P(None, ("tp", "fsdp"))
    tall = P("tp", "fsdp")
    return jax.shard_map(
        build(mesh.shape["fsdp"], mesh.shape["tp"]),
        mesh=mesh,
        in_specs=(rows, gains, wide, taps, tall, gains, wide, tall, rows, P()),
        out_specs=(rows, rows, gains, wide, taps, tall, gains, wide, tall, P("fsdp", "tp")),
        check_vma=False,
    )
```

```python
import jax
import jax.numpy as jnp
from jax import lax
from jax.experimental import pallas as pl
from jax.experimental.layout import Layout, with_layout_constraint
from jax.experimental.pallas import tpu as pltpu
from jax.sharding import PartitionSpec as P


EPSILON = 1e-05
F32 = jnp.float32
BF16 = jnp.bfloat16


def flip(value, axis, size, mask):
    return lax.ppermute(value, axis, [(i, i ^ mask) for i in range(size)])


def bits_of(size):
    return [1 << b for b in range(size.bit_length() - 1)]


def gather_small(value, axis, size):
    value = value[None]
    index = lax.axis_index(axis)
    for bit in bits_of(size):
        other = flip(value, axis, size, bit)
        high = (index & bit) != 0
        value = jnp.where(
            high, jnp.concatenate([other, value], 0), jnp.concatenate([value, other], 0)
        )
    return value


def gather_direct(value, axis, size):
    index = lax.axis_index(axis)
    copies = [value] + [flip(value, axis, size, m) for m in range(1, size)]
    places = jnp.arange(size) ^ index
    return sum(
        jnp.where((places == m)[:, None], copies[m][None], 0.0) for m in range(size)
    )


def scatter_direct(value, axis, size):
    index = lax.axis_index(axis)
    places = jnp.arange(size) ^ index

    def row(m):
        return jnp.sum(jnp.where((places == m)[:, None], value, 0.0), axis=0)

    return row(0) + sum(flip(row(m), axis, size, m) for m in range(1, size))


def scatter_small(value, axis, size):
    index = lax.axis_index(axis)
    for bit in reversed(bits_of(size)):
        half = value.shape[0] // 2
        high = (index & bit) != 0
        mine = jnp.where(high, value[half:], value[:half])
        other = jnp.where(high, value[:half], value[half:])
        value = mine + flip(other, axis, size, bit)
    return value[0]


def spread(piece, size, late=None):
    half = piece.shape[0] // 2
    if size == 4:
        top, low = piece[:half], piece[half:]
        x_top = flip(top, "tp", size, 1)
        y_low = flip(low, "tp", size, 2)
        x_low = flip(low, "tp", size, 1)
        y_top = flip(top, "tp", size, 2)
        send_top, send_low = x_top, y_low
        if late is not None:
            send_top, send_low = after(late(), send_top, send_low)
        far_top = flip(send_top, "tp", size, 2)
        far_low = flip(send_low, "tp", size, 1)
        return [(top, low), (x_top, x_low), (y_top, y_low), (far_top, far_low)]
    held = {0: piece}
    for bit in bits_of(size):
        for mask in sorted(held):
            held[mask | bit] = flip(held[mask], "tp", size, bit)
    return [held[m] for m in range(size)]


def last_of(pieces):
    return pieces_of(pieces[-1])[-1]


def collect_rows(parts, size):
    held = {m: parts[m] for m in range(size)}
    for bit in reversed(bits_of(size)):
        for mask in [m for m in sorted(held) if m & bit]:
            got = flip(held.pop(mask), "tp", size, bit)
            low = mask ^ bit
            held[low] = (held[low].astype(F32) + got.astype(F32)).astype(BF16)
    return held[0].astype(F32)


def collect_pairs(first, second, own):
    (send_x, rest_y), (send_y, rest_x) = first, second
    rows, half = rest_y.shape
    got_x = flip(send_x, "tp", 4, 1)
    got_y = flip(send_y, "tp", 4, 2)
    next_y = (rest_y.astype(F32) + got_x[:rows].astype(F32)).astype(BF16)
    next_x = (rest_x.astype(F32) + got_y[:rows].astype(F32)).astype(BF16)
    next_y, next_x = lax.optimization_barrier((next_y, next_x))
    last_y = flip(next_y, "tp", 4, 2)
    last_x = flip(next_x, "tp", 4, 1)
    last_y, last_x = lax.optimization_barrier((last_y, last_x))
    left = own[:, :half].astype(F32) + got_x[rows:].astype(F32) + last_y.astype(F32)
    right = own[:, half:].astype(F32) + got_y[rows:].astype(F32) + last_x.astype(F32)
    return jnp.concatenate([left, right], axis=1)


def dot_rows(left, right):
    return lax.dot_general(left, right, (((0,), (0,)), ((), ())), preferred_element_type=F32)


def dot_cols(left, right):
    return lax.dot_general(left, right, (((1,), (1,)), ((), ())), preferred_element_type=F32)


def planes(value):
    return with_layout_constraint(value, Layout(major_to_minor=(1, 0, 2)))


VMEM_MOST = 60 * 1024 * 1024
VMEM_MID = 44 * 1024 * 1024
VMEM_LESS = 40 * 1024 * 1024


def hidden_tile(size):
    return size if size <= 896 else 896


def width_tile(size, most):
    tile = most
    while size % tile:
        tile -= 128
    return tile


def call(body, grid, ins, outs, flops, operands, aliases=None, limit=VMEM_LESS):
    moved = sum(v.size * v.dtype.itemsize for v in operands)
    return pl.pallas_call(
        body,
        grid=grid,
        in_specs=ins,
        out_specs=[spec for spec, _ in outs],
        out_shape=[shape for _, shape in outs],
        input_output_aliases=aliases or {},
        compiler_params=pltpu.CompilerParams(vmem_limit_bytes=limit),
        cost_estimate=pl.CostEstimate(flops=flops, bytes_accessed=moved, transcendentals=0),
    )(*operands)


def stacked(refs):
    parts = [r[...] for r in refs]
    return parts[0] if len(parts) == 1 else jnp.concatenate(parts, axis=0)


def pieces_of(part):
    return part if isinstance(part, tuple) else (part,)


def gate_up_kernel(parts, weights, place, total, before):
    rows, width = sum(v.shape[0] for v in parts), parts[0].shape[1]
    hidden = weights.shape[2]
    tile = hidden_tile(hidden)
    n = len(parts)

    def body(*refs):
        gate_ref, up_ref, act_ref = refs[-3:]
        rows_in = stacked(refs[:n])
        gate = jnp.dot(rows_in, refs[n][...], preferred_element_type=F32)
        up = jnp.dot(rows_in, refs[n + 1][...], preferred_element_type=F32)
        sig = jax.nn.sigmoid(gate)
        silu = gate * sig
        gate_ref[...] = (up * sig * (1.0 + gate * (1.0 - sig))).astype(BF16)
        up_ref[...] = silu.astype(BF16)
        act_ref[...] = (silu * up).astype(BF16)

    ins = [pl.BlockSpec(v.shape, lambda j: (0, 0)) for v in parts]
    ins += [
        pl.BlockSpec((None, width, tile), lambda j: (0, 0, j)),
        pl.BlockSpec((None, width, tile), lambda j: (1, 0, j)),
    ]
    ins += [pl.BlockSpec(memory_space=pl.ANY)] * len(before)
    shape = jax.ShapeDtypeStruct((total, hidden), BF16)
    outs = [(pl.BlockSpec((rows, tile), lambda j: (place, j)), shape)] * 3
    aliases = {n + 2 + i: i for i in range(len(before))}
    return call(
        body,
        (pl.cdiv(hidden, tile),),
        ins,
        outs,
        4 * rows * width * hidden,
        [*parts, weights, weights, *before],
        aliases,
        VMEM_MOST,
    )


def act_back_kernel(parts, weights, gate, up):
    count, (width, hidden) = 2, weights.shape
    each = len(parts) // count
    flat = [(m // each, v) for m, part in enumerate(parts) for v in pieces_of(part)]
    total = gate.shape[0]
    rows = total // count
    tile = hidden_tile(hidden)
    n = len(flat)

    def body(*refs):
        weight_ref, gate_ref, up_ref, out_ref, held, sems = refs[n:]
        turn, place = pl.program_id(0), pl.program_id(1)
        copies, at = [], 0
        for i, (m, v) in enumerate(flat):
            copies.append(
                pltpu.make_async_copy(refs[i], held.at[pl.ds(at, v.shape[0])], sems.at[i])
            )
            at += v.shape[0]

        @pl.when((turn == 0) & (place == 0))
        def _():
            for copy in copies:
                copy.start()

        for m in range(count):

            @pl.when((turn == 0) & (place == m))
            def _():
                for (owner, _), copy in zip(flat, copies):
                    if owner == m:
                        copy.wait()

        rows_in = held[pl.ds(pl.multiple_of(place * rows, rows), rows)]
        back = jnp.dot(rows_in, weight_ref[...], preferred_element_type=F32)
        out_ref[0] = (back * gate_ref[...].astype(F32)).astype(BF16)
        out_ref[1] = (back * up_ref[...].astype(F32)).astype(BF16)

    block = pl.BlockSpec((rows, tile), lambda j, i: (i, j))
    operands = [v for _, v in flat] + [weights, gate, up]
    return pl.pallas_call(
        body,
        name="ab",
        grid=(pl.cdiv(hidden, tile), count),
        in_specs=[pl.BlockSpec(memory_space=pl.ANY)] * n
        + [pl.BlockSpec((width, tile), lambda j, i: (0, j)), block, block],
        out_specs=pl.BlockSpec((2, rows, tile), lambda j, i: (0, i, j)),
        out_shape=jax.ShapeDtypeStruct((2, total, hidden), BF16),
        scratch_shapes=[pltpu.VMEM((total, width), BF16), pltpu.SemaphoreType.DMA((n,))],
        compiler_params=pltpu.CompilerParams(vmem_limit_bytes=VMEM_MID),
        cost_estimate=pl.CostEstimate(
            flops=2 * total * width * hidden,
            bytes_accessed=sum(v.size * v.dtype.itemsize for v in operands),
            transcendentals=0,
        ),
    )(*operands)


def chosen(index, table):
    value = table[-1]
    for n, entry in enumerate(table[:-1]):
        value = jnp.where(index == n, entry, value)
    return value


def back_kernel(grads, weights, rows, places, part=0, parts=1, split=0):
    planes_of, _, hidden = grads.shape
    cols = weights.shape[1] // parts
    tile = width_tile(cols, 768)
    steps = cols // tile
    count = len(places)

    def body(grad_ref, weight_ref, *out_refs):
        value = sum(dot_cols(grad_ref[k], weight_ref[k]) for k in range(planes_of)).astype(BF16)
        if split == 0:
            out_refs[0][...] = value
        else:
            place = pl.program_id(1)

            @pl.when(place < split)
            def _():
                out_refs[0][...] = value

            @pl.when(place >= split)
            def _():
                out_refs[1][...] = value

    ins = [
        pl.BlockSpec((planes_of, rows, hidden), lambda j, i: (0, chosen(i, places), 0)),
        pl.BlockSpec((planes_of, tile, hidden), lambda j, i: (0, part * steps + j, 0)),
    ]

    def out(blocks, at):
        shape = jax.ShapeDtypeStruct((blocks * rows, cols), BF16)
        return pl.BlockSpec((rows, tile), lambda j, i: (at(i), j)), shape

    if split == 0:
        outs = [out(count, lambda i: i)]
    else:
        outs = [
            out(split, lambda i: jnp.minimum(i, split - 1)),
            out(count - split, lambda i: jnp.maximum(i - split, 0)),
        ]
    flops = 2 * planes_of * count * rows * cols * hidden
    made = call(body, (steps, count), ins, outs, flops, [grads, weights])
    return made[0] if split == 0 else made


def sum_kernel(parts, grads, limit=VMEM_LESS):
    flat = [v for part in parts for v in pieces_of(part)]
    width = flat[0].shape[1]
    planes_of, total, hidden = grads.shape
    tile = width_tile(width, 768)
    across = hidden_tile(hidden)
    n = len(flat)

    def body(*refs):
        refs[n + 1][...] = dot_rows(stacked(refs[:n]), refs[n][...]).astype(BF16)

    ins = [pl.BlockSpec((v.shape[0], tile), lambda i, k, j: (0, i)) for v in flat]
    ins += [pl.BlockSpec((None, total, across), lambda i, k, j: (k, 0, j))]
    outs = [
        (
            pl.BlockSpec((None, tile, across), lambda i, k, j: (k, i, j)),
            jax.ShapeDtypeStruct((planes_of, width, hidden), BF16),
        )
    ]
    grid = (width // tile, planes_of, pl.cdiv(hidden, across))
    flops = 2 * total * width * hidden * planes_of
    operands = [*flat, grads]
    return call(body, grid, ins, outs, flops, operands, None, limit)[0]


def column_kernel(parts, grads, width_out, block, before=(), addend=None, kind=BF16):
    flat = [v for part in parts for v in pieces_of(part)]
    width = flat[0].shape[1]
    total, cols = grads.shape
    tile = width_tile(width, 768)
    n = len(flat)

    def body(*refs):
        value = dot_rows(stacked(refs[:n]), refs[n][...])
        if addend is not None:
            value = value + refs[n + 1][...]
        refs[-1][...] = value.astype(kind)

    ins = [pl.BlockSpec((v.shape[0], tile), lambda i: (0, i)) for v in flat]
    ins += [pl.BlockSpec((total, cols), lambda i: (0, 0))]
    added = [] if addend is None else [addend]
    ins += [pl.BlockSpec((tile, cols), lambda i: (i, 0))] * len(added)
    ins += [pl.BlockSpec(memory_space=pl.ANY)] * len(before)
    outs = [
        (
            pl.BlockSpec((tile, cols), lambda i: (i, block)),
            jax.ShapeDtypeStruct((width, width_out), kind),
        )
    ]
    flops = 2 * total * width * cols
    aliases = {n + 1 + len(added): 0} if before else {}
    operands = [*flat, grads, *added, *before]
    return call(body, (width // tile,), ins, outs, flops, operands, aliases)[0]


def fetch(refs, sizes, held, sems):
    copies, at = [], 0
    for i, size in enumerate(sizes):
        copies.append(pltpu.make_async_copy(refs[i], held.at[pl.ds(at, size)], sems.at[i]))
        at += size
    for copy in copies:
        copy.start()
    for copy in copies:
        copy.wait()


def shifted(value, steps, edges):
    count = value.shape[0]
    moved = pltpu.roll(value, steps % count, 0)
    row = lax.broadcasted_iota(jnp.int32, value.shape, 0)
    places = range(steps) if steps > 0 else range(count + steps, count)
    for place, edge in zip(places, edges):
        moved = jnp.where(row == place, edge, moved)
    return moved


def front_kernel(order, parts, gain, weights, taps, rows):
    flat = [v for part in parts for v in pieces_of(part)]
    sizes = [v.shape[0] for v in flat]
    total, width = sum(sizes), flat[0].shape[1]
    channels = weights.shape[1] // 4
    wide = 3 * channels
    count = total // rows
    n = len(flat)

    def body(order_ref, *refs):
        gain_ref, w_ref, taps_ref = refs[n : n + 3]
        x_ref, kept_ref, edge_ref, gated_ref, out_ref, held, carry, sems = refs[n + 3 :]
        step = pl.program_id(0)

        @pl.when(step == 0)
        def _():
            carry[...] = jnp.zeros_like(carry)
            fetch(refs[:n], sizes, held, sems)

        at = pl.multiple_of(order_ref[step] * rows, rows)
        x = (held[pl.ds(at, rows)].astype(F32) * gain_ref[...]).astype(BF16)
        x_ref[...] = x
        made = jnp.dot(x, w_ref[:, :wide], preferred_element_type=F32)
        kept_ref[...] = made
        input_gate, output_gate, inner = (
            made[:, k * channels : (k + 1) * channels] for k in range(3)
        )
        mixed = input_gate * inner
        edge = carry[...]
        edge_ref[...] = edge
        one = shifted(mixed, 1, [edge[1:2]])
        two = shifted(mixed, 2, [edge[0:1], edge[1:2]])
        carry[0:2] = mixed[rows - 2 :]
        conv = taps_ref[0:1] * two + taps_ref[1:2] * one + taps_ref[2:3] * mixed
        gated = (output_gate * conv).astype(BF16)
        gated_ref[...] = gated
        out_ref[...] = dot_cols(gated, w_ref[:, wide:]).astype(BF16)

    specs = pltpu.PrefetchScalarGridSpec(
        num_scalar_prefetch=1,
        grid=(count,),
        in_specs=[
            *([pl.BlockSpec(memory_space=pl.ANY)] * n),
            pl.BlockSpec((1, width), lambda p, order: (0, 0)),
            pl.BlockSpec(weights.shape, lambda p, order: (0, 0)),
            pl.BlockSpec(taps.shape, lambda p, order: (0, 0)),
        ],
        out_specs=[
            pl.BlockSpec((rows, width), lambda p, order: (order[p], 0)),
            pl.BlockSpec((rows, wide), lambda p, order: (order[p], 0)),
            pl.BlockSpec((None, 8, channels), lambda p, order: (order[p], 0, 0)),
            pl.BlockSpec((rows, channels), lambda p, order: (order[p], 0)),
            pl.BlockSpec((rows, width), lambda p, order: (order[p], 0)),
        ],
        scratch_shapes=[
            pltpu.VMEM((total, width), BF16),
            pltpu.VMEM((8, channels), F32),
            pltpu.SemaphoreType.DMA((n,)),
        ],
    )
    return pl.pallas_call(
        body,
        name="cf",
        grid_spec=specs,
        out_shape=[
            jax.ShapeDtypeStruct((total, width), BF16),
            jax.ShapeDtypeStruct((total, wide), F32),
            jax.ShapeDtypeStruct((count, 8, channels), F32),
            jax.ShapeDtypeStruct((total, channels), BF16),
            jax.ShapeDtypeStruct((total, width), BF16),
        ],
        compiler_params=pltpu.CompilerParams(vmem_limit_bytes=VMEM_LESS),
        cost_estimate=pl.CostEstimate(
            flops=8 * total * width * channels,
            bytes_accessed=4 * total * (width + 4 * channels) + 8 * width * channels,
            transcendentals=0,
        ),
    )(order, *flat, gain[None], weights, taps)


def conv_back_kernel(order, parts, weights, taps, kept, edges, rows):
    flat = [v for part in parts for v in pieces_of(part)]
    sizes = [v.shape[0] for v in flat]
    total, width = sum(sizes), flat[0].shape[1]
    channels = weights.shape[1] // 4
    wide = 3 * channels
    count = total // rows
    n = len(flat)
    out_cols, out_block = (channels, 3) if channels % 128 == 0 else (4 * channels, 0)

    def body(order_ref, *refs):
        w_ref, taps_ref, kept_ref, edge_ref, out_ref, sums_ref, held, carry, sems = refs[n:]
        step = pl.program_id(0)

        @pl.when(step == 0)
        def _():
            carry[...] = jnp.zeros_like(carry)
            sums_ref[...] = jnp.zeros_like(sums_ref)
            fetch(refs[:n], sizes, held, sems)

        at = pl.multiple_of(order_ref[count - 1 - step] * rows, rows)
        out_weight = w_ref[:, out_cols - channels :]
        back = jnp.dot(held[pl.ds(at, rows)], out_weight, preferred_element_type=F32)
        input_gate, output_gate, inner = (
            kept_ref[:, k * channels : (k + 1) * channels] for k in range(3)
        )
        mixed = input_gate * inner
        edge = edge_ref[...]
        one = shifted(mixed, 1, [edge[1:2]])
        two = shifted(mixed, 2, [edge[0:1], edge[1:2]])
        conv = taps_ref[0:1] * two + taps_ref[1:2] * one + taps_ref[2:3] * mixed
        out_ref[:, channels : 2 * channels] = (back * conv).astype(BF16)
        grad = back * output_gate
        sums_ref[0:1] += jnp.sum(grad * two, axis=0, keepdims=True)
        sums_ref[1:2] += jnp.sum(grad * one, axis=0, keepdims=True)
        sums_ref[2:3] += jnp.sum(grad * mixed, axis=0, keepdims=True)
        head = carry[...]
        later_one = shifted(grad, -1, [head[0:1]])
        later_two = shifted(grad, -2, [head[0:1], head[1:2]])
        carry[0:2] = grad[0:2]
        back_mixed = taps_ref[2:3] * grad + taps_ref[1:2] * later_one + taps_ref[0:1] * later_two
        out_ref[:, :channels] = (back_mixed * inner).astype(BF16)
        out_ref[:, 2 * channels :] = (back_mixed * input_gate).astype(BF16)

    specs = pltpu.PrefetchScalarGridSpec(
        num_scalar_prefetch=1,
        grid=(count,),
        in_specs=[
            *([pl.BlockSpec(memory_space=pl.ANY)] * n),
            pl.BlockSpec((width, out_cols), lambda p, order: (0, out_block)),
            pl.BlockSpec(taps.shape, lambda p, order: (0, 0)),
            pl.BlockSpec((rows, wide), lambda p, order: (order[count - 1 - p], 0)),
            pl.BlockSpec((None, 8, channels), lambda p, order: (order[count - 1 - p], 0, 0)),
        ],
        out_specs=[
            pl.BlockSpec((rows, wide), lambda p, order: (order[count - 1 - p], 0)),
            pl.BlockSpec((8, channels), lambda p, order: (0, 0)),
        ],
        scratch_shapes=[
            pltpu.VMEM((total, width), BF16),
            pltpu.VMEM((8, channels), F32),
            pltpu.SemaphoreType.DMA((n,)),
        ],
    )
    return pl.pallas_call(
        body,
        name="cb",
        grid_spec=specs,
        out_shape=[
            jax.ShapeDtypeStruct((total, wide), BF16),
            jax.ShapeDtypeStruct((8, channels), F32),
        ],
        compiler_params=pltpu.CompilerParams(vmem_limit_bytes=VMEM_LESS),
        cost_estimate=pl.CostEstimate(
            flops=2 * total * width * channels,
            bytes_accessed=2 * total * (width + 9 * channels) + 2 * width * channels,
            transcendentals=0,
        ),
    )(order, *flat, weights, taps, kept, edges)


def after(done, *values):
    held = lax.optimization_barrier((done,) + values)
    return held[1] if len(values) == 1 else held[1:]


def build(n_f, n_tp):
    def block(
        tokens,
        gain_one,
        in_weight,
        conv_weight,
        out_weight,
        gain_two,
        gate_up_weight,
        down_weight,
        cotangent,
        lengths,
    ):
        rows, width = tokens.shape
        channels = in_weight.shape[2]
        gain_width = gain_one.shape[0]
        tp_index = lax.axis_index("tp")

        wide = 3 * channels
        io_local = jnp.concatenate([in_weight.reshape(-1, wide), out_weight.T], axis=1)
        weight_io = lax.all_gather(io_local, "fsdp", axis=0, tiled=True)
        weight_gu = planes(lax.all_gather(planes(gate_up_weight), "fsdp", axis=0, tiled=True))
        weight_down = lax.all_gather(down_weight, "fsdp", axis=1, tiled=True)

        inputs = tokens.astype(F32)
        scale_one = lax.rsqrt(jnp.mean(inputs * inputs, axis=1, keepdims=True) + EPSILON)
        plain = (inputs * scale_one).astype(BF16)
        plain_parts = spread(plain, n_tp)

        small = jnp.concatenate([gain_one, gain_two, conv_weight.astype(F32).reshape(-1)])
        small = gather_small(small, "fsdp", n_f)
        taps = (
            small[:, 2 * gain_width :]
            .reshape(n_f, 3, gain_width)
            .transpose(1, 0, 2)
            .reshape(3, channels)
        )
        gains = gather_direct(small[:, : 2 * gain_width].reshape(-1), "tp", n_tp)
        gains = gains.reshape(n_tp, n_f, 2, gain_width).transpose(2, 1, 0, 3).reshape(2, width)
        gain_first, gain_second = gains[0], gains[1]

        length = lengths[lax.axis_index("fsdp")]
        position = tp_index * rows + jnp.arange(rows)
        valid_mask = (position < length).astype(F32)[:, None]
        grad_ffn = cotangent.astype(F32) * valid_mask
        cot_piece = grad_ffn.astype(BF16)

        order = tp_index.astype(jnp.int32) ^ jnp.arange(n_tp, dtype=jnp.int32)
        paired = n_tp == 4
        wide_gu = weight_gu.swapaxes(0, 1)
        wide_down = weight_down.T

        def rows_of(value, m):
            return value[m * rows : (m + 1) * rows]

        def shared_sum(grads, weights, place, between=None, late=None, extras=(), middle_of=None):
            if not paired:
                every = back_kernel(grads, weights, rows, place)
                middle = middle_of(every) if middle_of else every
                middle = between(middle) if between else middle
                every = after(late if late is not None else middle, every)
                total = collect_rows([rows_of(every, m) for m in range(n_tp)], n_tp)
                return total, list(extras)
            left = back_kernel(grads, weights, rows, [place[3], place[1], place[2]], 0, 2, 2)
            ready = middle_of(left[0]) if middle_of else left[0]
            right = back_kernel(
                after(ready, grads), weights, rows, [place[3], place[2], place[1]], 1, 2, 2
            )
            middle = between(right[0]) if between else right[0]
            if extras:
                extras = after(middle, *extras)
                held = lax.optimization_barrier((middle, *extras, grads))
                extras, late_grads = held[1:-1], held[-1]
            else:
                late_grads = after(middle, grads)
            own = back_kernel(late_grads, weights, rows, [place[0]])
            if late is not None:
                left = tuple(after(late, *left))
                right = tuple(after(late, *right))
            return collect_pairs(left, right, own), list(extras)

        gathered, projected, edges, gated, branch = front_kernel(
            order, plain_parts, gain_first, weight_io, taps, rows
        )
        branch_parts = [rows_of(branch, m) for m in range(n_tp)]
        if paired:
            half = width // 2
            own, near_x, near_y, far = branch_parts
            branch_sum = collect_pairs(
                (jnp.concatenate([far[:, :half], near_x[:, :half]]), near_y[:, :half]),
                (jnp.concatenate([far[:, half:], near_y[:, half:]]), near_x[:, half:]),
                own,
            )
        else:
            branch_sum = collect_rows(branch_parts, n_tp)
        hidden = inputs + branch_sum
        scale_two = lax.rsqrt(jnp.mean(hidden * hidden, axis=1, keepdims=True) + EPSILON)
        normed_two = (hidden * scale_two * gain_second).astype(BF16)
        parts_two = spread(normed_two, n_tp)
        cot_parts = spread(cot_piece, n_tp)

        stand = [1, 2, 0, 3] if paired else list(range(n_tp))
        place = [stand.index(m) for m in range(n_tp)]
        parts_two = [parts_two[m] for m in stand]
        cot_parts = [cot_parts[m] for m in stand]
        groups = [([2], 2), ([0, 1], 0), ([3], 3)] if paired else [([m], m) for m in range(n_tp)]
        kept = ()
        for members, at in groups:
            flat = [v for m in members for v in pieces_of(parts_two[m])]
            kept = gate_up_kernel(flat, wide_gu, at, n_tp * rows, kept)
        gate_part, up_part, activated = kept

        down_local = sum_kernel(cot_parts, activated[None], VMEM_MOST)[0]
        down_turned = with_layout_constraint(down_local.T, Layout(major_to_minor=(1, 0)))
        down_grad = lax.psum_scatter(down_turned, "fsdp", scatter_dimension=1, tiled=True)
        down_grad = down_grad.astype(F32)

        late_gate, late_up, late_down = after(down_local, gate_part, up_part, wide_down)
        grads = act_back_kernel(cot_parts, late_down, late_gate, late_up)

        def gate_up_sum(done):
            return sum_kernel(parts_two, after(done, grads))

        made = []

        def gate_up_once(done):
            made.append(gate_up_sum(done))
            return made[0]

        grad_normed_two, _ = shared_sum(grads, wide_gu, place, gate_up_once)
        gate_up_local = made[0]
        gate_up_turned = planes(gate_up_local.swapaxes(0, 1))
        gate_up_grad = lax.psum_scatter(
            gate_up_turned, "fsdp", scatter_dimension=0, tiled=True
        )
        gate_up_grad = gate_up_grad.astype(F32)

        weighted = grad_normed_two * gain_second
        inner_mean = jnp.mean(weighted * hidden, axis=1, keepdims=True)
        gain_two_local = jnp.sum(grad_normed_two * hidden * scale_two, axis=0)
        grad_hidden = (
            grad_ffn + scale_two * weighted - hidden * (scale_two * scale_two * scale_two) * inner_mean
        )
        branch_piece = grad_hidden.astype(BF16)
        grad_parts = spread(branch_piece, n_tp)

        ffn_total, _ = shared_sum(
            after(branch_piece, activated)[None], wide_down[None], place, late=last_of(grad_parts)
        )
        full_out = hidden + ffn_total
        output = full_out.astype(BF16)
        squares = jnp.sum(full_out * full_out * valid_mask, axis=0)

        near_rows = (n_tp - 1) * rows
        out_near = column_kernel(grad_parts[:-1], gated[:near_rows], channels, 0, (), None, F32)
        far_parts, gated_far = grad_parts[-1:], gated[near_rows:]
        grads_io, tap_sums = conv_back_kernel(
            order, grad_parts, weight_io, taps, projected, edges, rows
        )
        conv_local = tap_sums[:3]
        aligned = channels % 128 == 0
        weight_in = weight_io if aligned else weight_io[:, :wide]
        sums = []

        def io_sums(done):
            late_grads = after(done, grads_io)
            if aligned:
                io_sum = column_kernel([gathered], late_grads, 4 * channels, 0)
            else:
                io_sum = column_kernel([gathered], late_grads, wide, 0)
            if aligned:
                io_sum = column_kernel(far_parts, gated_far, 4 * channels, 3, (io_sum,), out_near)
            else:
                out_far = column_kernel(far_parts, gated_far, channels, 0, (), out_near)
                io_sum = jnp.concatenate([io_sum, out_far], axis=1)
            sums.append(io_sum)
            return io_sum

        def gain_of(done):
            late_sum = after(done, sums[0])
            product = late_sum[:, :wide].astype(F32) * weight_io[:, :wide].astype(F32)
            sums.append(jnp.sum(product, axis=1) / gain_first)
            return done

        grad_normed, (gate_up_grad, down_grad, output) = shared_sum(
            grads_io[None],
            weight_in[None],
            list(range(n_tp)),
            lambda done: gain_of(io_sums(done)),
            extras=(gate_up_grad, down_grad, output),
        )
        io_sum, gain_one_local = sums
        io_grad = lax.psum_scatter(io_sum, "fsdp", scatter_dimension=0, tiled=True)
        io_grad = io_grad.astype(F32)
        in_grad, out_grad = io_grad[:, :wide].reshape(-1, 3, channels), io_grad[:, wide:].T
        late_two, late_conv = after(io_sum, gain_two_local, conv_local)
        conv_share = late_conv.reshape(3, n_f, -1).transpose(1, 0, 2).reshape(n_f, -1)
        small_sums = jnp.concatenate(
            [gain_one_local.reshape(n_f, -1), late_two.reshape(n_f, -1), conv_share], axis=1
        )
        small_sums = scatter_small(small_sums, "fsdp", n_f)
        share = width // n_f
        conv_grad = small_sums[2 * share :].reshape(3, -1)
        small_sums = jnp.concatenate(
            [
                small_sums[:share].reshape(n_tp, -1),
                small_sums[share : 2 * share].reshape(n_tp, -1),
                squares.reshape(n_tp, -1),
            ],
            axis=1,
        )
        small_sums = scatter_direct(small_sums, "tp", n_tp)
        gain_one_grad = small_sums[:gain_width]
        gain_two_grad = small_sums[gain_width : 2 * gain_width]
        out_rms = jnp.sqrt(small_sums[2 * gain_width :] / length.astype(F32))[None, :]
        weighted_one = grad_normed * gain_first
        inner_one = jnp.mean(weighted_one * inputs, axis=1, keepdims=True)
        input_grad = (
            grad_hidden
            + scale_one * weighted_one
            - inputs * (scale_one * scale_one * scale_one) * inner_one
        ).astype(BF16)

        return (
            output,
            input_grad,
            gain_one_grad,
            in_grad,
            conv_grad,
            out_grad,
            gain_two_grad,
            gate_up_grad,
            down_grad,
            out_rms,
        )

    return block


def solution(mesh):
    rows = P(("fsdp", "tp"), None)
    gains = P(("fsdp", "tp"))
    wide = P("fsdp", None, "tp")
    taps = P(None, ("tp", "fsdp"))
    tall = P("tp", "fsdp")
    return jax.shard_map(
        build(mesh.shape["fsdp"], mesh.shape["tp"]),
        mesh=mesh,
        in_specs=(rows, gains, wide, taps, tall, gains, wide, tall, rows, P()),
        out_specs=(rows, rows, gains, wide, taps, tall, gains, wide, tall, P("fsdp", "tp")),
        check_vma=False,
    )
```
